128 devices in a mesh: gx: 16 (over y, z_lo, core), gy: 8 (over x, z_hi).
Axes of the slice: x: 4, y: 4, z: 4 (z_hi: 2, z_lo: 2; z = z_hi * 2 + z_lo), core: 2. Of those that a mesh axis runs over, the one named last changes fastest.
Arguments:
- populations: float32 [19, 256, 256, 128], P(None, 'gx', 'gy'), may hold values from 0 to 10, as said below
- solid: int32 [256, 256, 128], P('gx', 'gy'), may hold values 0 or 1
Outputs:
- advanced: float32 [19, 256, 256, 128], P(None, 'gx', 'gy')
The draws below stay inside these ranges and needn't reach their ends.
Inputs may be any that keep to these rules, and one draw needn't show every extreme that they name: populations are positive, each between 0.5 w_i 18 and 1.5 w_i 18.
All inputs are finite; a program needn't handle non-finite values. No bound on the sum of `solid` on one device may be relied on, other than what follows from the above.
Results may differ from the reference program's by a relative error of at most 0.0001.
Values sent between devices are 32-bit elements; how exact they have to be, the bound alone decides.
No kernel may reach another device: no remote copies, remote signals or barrier semaphores. Data moves between devices by JAX's collectives and lax.ppermute only.
A program may use at most 128 MiB of HBM per device.

```python
import jax
import jax.numpy as jnp
import numpy as np
from jax import lax

NZ = 128
ITERS = 3
NX = 256
NY = 256


def draw_populations(key, part):
    weights = jnp.array([1.0 / 3.0] + [1.0 / 18.0] * 6 + [1.0 / 36.0] * 12, jnp.float32)
    rough = jax.random.uniform(key, (19, NX, NY, NZ), jnp.float32, -1.0, 1.0)
    factor = 1.0 + 0.45 * rough
    return (18.0 * weights[:, None, None, None] * factor).astype(jnp.float32)


def set_ends(entries, key, least, high):
    place = [jax.random.randint(jax.random.fold_in(key, axis), (), 0, length) for axis, length in enumerate(entries.shape)]
    widest = entries.shape.index(max(entries.shape))
    beside = place[:widest] + [(place[widest] + 1) % entries.shape[widest]] + place[widest + 1:]
    return entries.at[tuple(place)].set(least).at[tuple(beside)].set(high)


def setup_inputs(seed: int = 0) -> dict:
    key_of = jax.random.split(jax.random.key(seed), 3)
    populations = draw_populations(jax.random.fold_in(key_of[2], 71), 0)
    solid = set_ends((jax.random.randint(key_of[1], (NX, NY, NZ), 0, 8) < 1).astype(jnp.int32), jax.random.fold_in(key_of[1], 1), 0, 1)
    return {"populations": populations, "solid": solid}


velocity_table = np.array([[0, 0, 0], [1, 0, 0], [-1, 0, 0], [0, 1, 0], [0, -1, 0], [0, 0, 1], [0, 0, -1], [1, 1, 0], [-1, -1, 0], [1, -1, 0], [-1, 1, 0], [1, 0, 1], [-1, 0, -1], [1, 0, -1], [-1, 0, 1], [0, 1, 1], [0, -1, -1], [0, 1, -1], [0, -1, 1]])
weight_table = np.array([1.0 / 3.0] + [1.0 / 18.0] * 6 + [1.0 / 36.0] * 12)
relax = 1.6


def opposite(index):
    if index == 0:
        return 0
    return index + 1 if index % 2 == 1 else index - 1


def collide(field, fluid):
    table = jnp.asarray(velocity_table, jnp.float32)
    weights = jnp.asarray(weight_table, jnp.float32)
    density = jnp.sum(field, axis=0)
    moment = jnp.tensordot(table.T, field, axes=1, precision=lax.Precision.HIGHEST)
    speed = moment / density
    along = jnp.tensordot(table, speed, axes=1, precision=lax.Precision.HIGHEST)
    square = jnp.sum(speed * speed, axis=0)
    balance = weights[:, None, None, None] * density * (1.0 + 3.0 * along + 4.5 * along * along - 1.5 * square)
    return jnp.where(fluid, field + relax * (balance - field), field)


def reference(populations, solid):
    fluid = solid == 0
    field = populations
    for step in range(ITERS):
        post = collide(field, fluid)
        result = []
        for index in range(19):
            shift = tuple(int(v) for v in velocity_table[index])
            source = jnp.roll(post[index], shift, axis=(0, 1, 2))
            blocked = jnp.roll(solid, shift, axis=(0, 1, 2)) != 0
            value = jnp.where(blocked, post[opposite(index)], source)
            result.append(jnp.where(fluid, value, post[index]))
        field = jnp.stack(result)
    return field
```

```python
import jax
import jax.numpy as jnp
from jax import lax
from jax.experimental import pallas as pl
from jax.experimental.pallas import tpu as pltpu
from jax.sharding import PartitionSpec as P

ITERS = 3
NQ = 19
VEL = (
    (0, 0, 0),
    (1, 0, 0), (-1, 0, 0), (0, 1, 0), (0, -1, 0), (0, 0, 1), (0, 0, -1),
    (1, 1, 0), (-1, -1, 0), (1, -1, 0), (-1, 1, 0),
    (1, 0, 1), (-1, 0, -1), (1, 0, -1), (-1, 0, 1),
    (0, 1, 1), (0, -1, -1), (0, 1, -1), (0, -1, 1),
)
RELAX = 1.6
XP = tuple(i for i in range(NQ) if VEL[i][0] == 1)
XM = tuple(i for i in range(NQ) if VEL[i][0] == -1)
YP = tuple(i for i in range(NQ) if VEL[i][1] == 1)
YM = tuple(i for i in range(NQ) if VEL[i][1] == -1)
MARK = -float(2 ** 20)
EDGE = -1e5
FLAG_X = (0, 1, -1)


def opposite(i):
    if i == 0:
        return 0
    return i + 1 if i % 2 == 1 else i - 1


def collide(f):
    keep = 1.0 - RELAX
    d = {i: f[i] - f[i + 1] for i in range(1, NQ, 2)}
    s = [f[i] + f[i + 1] for i in range(1, NQ, 2)]
    rho = ((s[0] + s[1]) + (s[2] + s[3])) + ((s[4] + s[5]) + (s[6] + s[7])) + (s[8] + f[0])
    mx = (d[1] + d[7]) + (d[9] + d[11]) + d[13]
    my = (d[3] + d[7]) + (d[15] - d[9]) + d[17]
    mz = (d[5] + d[11]) + (d[15] - d[13]) - d[17]
    inv = 1.0 / rho
    ux, uy, uz = mx * inv, my * inv, mz * inv
    a, b, c = mx * ux, my * uy, mz * uz
    base = rho - 1.5 * ((a + b) + c)
    w0, w1, w2 = RELAX / 3.0, RELAX / 18.0, RELAX / 36.0
    post = [None] * NQ
    post[0] = keep * f[0] + w0 * base
    one, two = w1 * base, w2 * base

    def pair(i, even, odd):
        post[i] = keep * f[i] + (even + odd)
        post[i + 1] = keep * f[i + 1] + (even - odd)

    k1, o1 = 4.5 * w1, 3.0 * w1
    pair(1, one + k1 * a, o1 * mx)
    pair(3, one + k1 * b, o1 * my)
    pair(5, one + k1 * c, o1 * mz)
    k2, o2 = 4.5 * w2, 3.0 * w2
    qx, qy, qz = o2 * mx, o2 * my, o2 * mz
    ka, kb, kc = k2 * a, k2 * b, k2 * c
    kx, ky = (2.0 * k2) * mx, (2.0 * k2) * my
    for i, even, cross, p, q in (
        (7, two + (ka + kb), kx * uy, qx, qy),
        (11, two + (ka + kc), kx * uz, qx, qz),
        (15, two + (kb + kc), ky * uz, qy, qz),
    ):
        pair(i, even + cross, p + q)
        pair(i + 2, even - cross, p - q)
    return post


def send_faces(x, t, last_x, last_t, raw, xp, xm, yp, ym):
    fixed = isinstance(x, int)
    rows = pl.ds(8 * t, 8)
    if fixed and x == last_x:
        for k, v in enumerate(raw(XP)):
            xp[k, rows, :] = v
    if fixed and x == 0:
        for k, v in enumerate(raw(XM)):
            xm[k, rows, :] = v
    for side, ref, group, row in ((last_t, yp, YP, 7), (0, ym, YM, 0)):
        if t != side:
            continue
        steps = [VEL[i][0] for i in group] + list(FLAG_X)
        for k, v in enumerate(raw(group)):
            to = x + steps[k]
            if fixed and not 0 <= to <= last_x:
                continue
            ref[k, pl.ds(to, 1), :] = v[row:row + 1]


def even(axis):
    return lax.axis_index(axis) % 2 == 0


def by_edge(axis, up, down):
    first = even(axis)
    return jnp.where(first, up, down), jnp.where(first, down, up)


def columns(nx, body):
    body(0)

    def step(x, carry):
        body(x)
        return carry

    lax.fori_loop(1, nx - 1, step, 0)
    body(nx - 1)


def first_kernel(f_hbm, solid_hbm, post, x0, x1, yp, ym, xp, xm, solid, sem, solid_sem):
    nx, ny = post.shape[1], post.shape[2]
    parts = sem.shape[0]
    size = nx // parts
    flags = pltpu.make_async_copy(solid_hbm, solid, solid_sem)
    flags.start()
    copies = []
    for p in range(parts):
        at = pl.ds(p * size, size)
        copies.append(pltpu.make_async_copy(f_hbm.at[:, at], post.at[:, at], sem.at[p]))
        copies[-1].start()
    flags.wait()

    def body(x):
        for t in range(ny // 8):
            rows = pl.ds(8 * t, 8)
            f = [post[i, x, rows, :] for i in range(NQ)]
            new = collide(f)
            flag = solid[x, rows, :].astype(jnp.float32)
            blocked = flag > 0.5
            for i in range(NQ):
                post[i, x, rows, :] = jnp.where(blocked, f[i] * MARK, new[i])

            def raw(group):
                extra = [flag] * (3 if group in (YP, YM) else 1)
                return [new[i] for i in group] + extra

            send_faces(x, t, nx - 1, ny // 8 - 1, raw, xp, xm, yp, ym)

    def step(x, carry):
        body(x)
        return carry

    for p in range(parts):
        copies[p].wait()
        low, high = p * size, (p + 1) * size
        if p == 0:
            body(0)
            low = 1
        if p == parts - 1:
            high -= 1
        lax.fori_loop(low, high, step, 0)
        if p == parts - 1:
            body(nx - 1)
    order_faces(xp, xm, x0, x1)


def order_faces(xp, xm, x0, x1):
    for k in range(x0.shape[0]):
        x0[k], x1[k] = by_edge("gx", xp[k], xm[k])


def corner_kernel(yp, ym, r0, r1, y0, y1):
    nx, ny = yp.shape[1], r0.shape[1]
    row = lax.broadcasted_iota(jnp.int32, yp.shape[1:], 0)

    def filled(ref, k, group, end):
        step = VEL[group[k]][0] if k < 5 else FLAG_X[k - 5]
        cz = VEL[group[k]][2] if k < 5 else 0
        v = ref[k]
        if step == 0 or cz:
            return v
        side = XP if step == 1 else XM
        at = side.index(group[k]) if k < 5 else 5
        right, left = by_edge("gx", r0[at, end:end + 1], r1[at, end:end + 1])
        return jnp.where(row == (0 if step == 1 else nx - 1), left if step == 1 else right, v)

    for k in range(yp.shape[0]):
        y0[k], y1[k] = by_edge("gy", filled(yp, k, YP, ny - 1), filled(ym, k, YM, 0))


def mark_halos(r0, r1, s0, s1, flag_x0, flag_x1, flag_y0, flag_y1, hx, hy):
    flags = by_edge("gx", flag_x0[5], flag_x1[5])
    for k in range(5):
        values = by_edge("gx", r0[k], r1[k])
        for side in range(2):
            hx[side, k] = jnp.where(flags[1 - side] > 0.5, MARK, values[1 - side])
    for k in range(5):
        values = by_edge("gy", s0[k], s1[k])
        for side, group in enumerate((YP, YM)):
            plane = 5 + FLAG_X.index(VEL[group[k]][0])
            flag = by_edge("gy", flag_y0[plane], flag_y1[plane])[1 - side]
            hy[side, k] = jnp.where(flag > 0.5, MARK, values[1 - side])


def stream(post, hx, hy, x, t):
    nx, tiles = post.shape[1], post.shape[2] // 8
    fixed = isinstance(x, int)
    own = [post[i, x, pl.ds(8 * t, 8), :] for i in range(NQ)]
    row = lax.broadcasted_iota(jnp.int32, (8, 128), 0)
    f = [own[0]]
    for i in range(1, NQ):
        cx, cy, cz = VEL[i]
        if fixed and not 0 <= x - cx < nx:
            view = hx.at[0, XP.index(i)] if cx == 1 else hx.at[1, XM.index(i)]
        else:
            view = post.at[i, x - cx]
        if cy == 1 and t == 0:
            halo = jnp.broadcast_to(hy[0, YP.index(i), pl.ds(x, 1), :], (8, 128))
            v = jnp.where(row == 0, halo, pltpu.roll(view[pl.ds(0, 8), :], 1, 0))
        elif cy == -1 and t == tiles - 1:
            halo = jnp.broadcast_to(hy[1, YM.index(i), pl.ds(x, 1), :], (8, 128))
            v = jnp.where(row == 7, halo, pltpu.roll(view[pl.ds(8 * t, 8), :], 7, 0))
        else:
            v = view[pl.ds(8 * t - cy, 8), :]
        if cz:
            v = pltpu.roll(v, cz % 128, 1)
        f.append(jnp.where(v < EDGE, own[opposite(i)], v))
    return f, own, own[0] > EDGE


def middle_kernel(post, *refs):
    halos, (out, x0, x1, yp, ym, xp, xm, hx, hy) = refs[:8], refs[8:]
    nx, ny = post.shape[1], post.shape[2]
    mark_halos(*halos, hx, hy)

    def body(x):
        for t in range(ny // 8):
            rows = pl.ds(8 * t, 8)
            f, own, fluid = stream(post, hx, hy, x, t)
            new = collide(f)
            for i in range(NQ):
                out[i, x, rows, :] = jnp.where(fluid, new[i], own[i])
            send_faces(x, t, nx - 1, ny // 8 - 1, lambda group: [new[i] for i in group], xp, xm, yp, ym)

    columns(nx, body)
    order_faces(xp, xm, x0, x1)


def last_kernel(post, *refs):
    halos, (out_hbm, stage, hx, hy, sem) = refs[:8], refs[8:]
    nx, ny = post.shape[1], post.shape[2]
    mark_halos(*halos, hx, hy)

    def body(x):
        for t in range(ny // 8):
            f, own, fluid = stream(post, hx, hy, x, t)
            for i in range(NQ):
                stage[i, x, pl.ds(8 * t, 8), :] = jnp.where(fluid, f[i], own[i] * (1.0 / MARK))

    def step(x, carry):
        body(x)
        return carry

    parts = sem.shape[0]
    size = nx // parts
    copies = []
    for p in range(parts):
        begin, end = p * size, (p + 1) * size
        if p == 0:
            body(0)
            begin = 1
        if p == parts - 1:
            end -= 1
        lax.fori_loop(begin, end, step, 0)
        if p == parts - 1:
            body(nx - 1)
        at = pl.ds(p * size, size)
        copies.append(pltpu.make_async_copy(stage.at[:, at], out_hbm.at[:, at], sem.at[p]))
        copies[-1].start()
    for copy in copies:
        copy.wait()


def swap(value, axis, edge):
    count = lax.axis_size(axis)
    pairs = [((2 * j + edge) % count, (2 * j + edge + 1) % count) for j in range(count // 2)]
    return lax.ppermute(value, axis, pairs + [(b, a) for a, b in pairs])


def local(populations, solid):
    _, nx, ny, nz = populations.shape
    f32 = jnp.float32
    anywhere = pl.BlockSpec(memory_space=pl.ANY)
    onchip = pl.BlockSpec(memory_space=pltpu.VMEM)
    state = pltpu.VMEM(populations.shape, f32)
    params = pltpu.CompilerParams(vmem_limit_bytes=24 << 20)

    def faces(x_planes, y_planes):
        shape_x = jax.ShapeDtypeStruct((x_planes, ny, nz), f32)
        shape_y = jax.ShapeDtypeStruct((y_planes, nx, nz), f32)
        return (shape_x, shape_x, shape_y, shape_y)

    def exchange(x0, x1, yp, ym):
        r0, r1 = swap(x0, "gx", 0), swap(x1, "gx", 1)
        shape = jax.ShapeDtypeStruct(yp.shape, f32)
        y0, y1 = pl.pallas_call(
            corner_kernel,
            out_shape=(shape, shape),
            in_specs=[onchip] * 4,
            out_specs=(onchip,) * 2,
            compiler_params=params,
            name="corners",
        )(yp, ym, r0, r1)
        return r0, r1, swap(y0, "gy", 0), swap(y1, "gy", 1)

    post, *out = pl.pallas_call(
        first_kernel,
        out_shape=(state,) + faces(6, 8),
        in_specs=[anywhere, anywhere],
        out_specs=(onchip,) * 5,
        scratch_shapes=[pltpu.VMEM((6, ny, nz), f32)] * 2 + [
            pltpu.VMEM(solid.shape, jnp.int32),
            pltpu.SemaphoreType.DMA((4,)),
            pltpu.SemaphoreType.DMA,
        ],
        compiler_params=params,
        name="first",
    )(
        pltpu.with_memory_space_constraint(populations, pltpu.HBM),
        pltpu.with_memory_space_constraint(solid, pltpu.HBM),
    )
    halos = exchange(*out)
    flags = halos
    marked = [pltpu.VMEM((2, 5, ny, nz), f32), pltpu.VMEM((2, 5, nx, nz), f32)]
    for _ in range(ITERS - 1):
        post = pltpu.with_memory_space_constraint(post, pltpu.VMEM)
        post, *out = pl.pallas_call(
            middle_kernel,
            out_shape=(state,) + faces(5, 5),
            in_specs=[onchip] * 9,
            out_specs=(onchip,) * 5,
            scratch_shapes=[pltpu.VMEM((5, ny, nz), f32)] * 2 + marked,
            compiler_params=params,
            name="middle",
        )(post, *halos, *flags)
        halos = exchange(*out)
    post = pltpu.with_memory_space_constraint(post, pltpu.VMEM)
    return pl.pallas_call(
        last_kernel,
        out_shape=jax.ShapeDtypeStruct(populations.shape, f32),
        in_specs=[onchip] * 9,
        out_specs=anywhere,
        scratch_shapes=[pltpu.VMEM(populations.shape, f32)] + marked + [pltpu.SemaphoreType.DMA((4,))],
        compiler_params=params,
        name="last",
    )(post, *halos, *flags)


def solution(mesh):
    in_specs = (P(None, "gx", "gy", None), P("gx", "gy", None))
    out_specs = P(None, "gx", "gy", None)
    return jax.shard_map(local, mesh=mesh, in_specs=in_specs, out_specs=out_specs, check_vma=False)
```

```python
import jax
import jax.numpy as jnp
from jax import lax
from jax.experimental import pallas as pl
from jax.experimental.pallas import tpu as pltpu
from jax.sharding import PartitionSpec as P

ITERS = 3
NQ = 19
VEL = (
    (0, 0, 0),
    (1, 0, 0), (-1, 0, 0), (0, 1, 0), (0, -1, 0), (0, 0, 1), (0, 0, -1),
    (1, 1, 0), (-1, -1, 0), (1, -1, 0), (-1, 1, 0),
    (1, 0, 1), (-1, 0, -1), (1, 0, -1), (-1, 0, 1),
    (0, 1, 1), (0, -1, -1), (0, 1, -1), (0, -1, 1),
)
RELAX = 1.6
XP = tuple(i for i in range(NQ) if VEL[i][0] == 1)
XM = tuple(i for i in range(NQ) if VEL[i][0] == -1)
YP = tuple(i for i in range(NQ) if VEL[i][1] == 1)
YM = tuple(i for i in range(NQ) if VEL[i][1] == -1)
MARK = -float(2 ** 20)
EDGE = -1e5
FLAG_X = (0, 1, -1)


def opposite(i):
    if i == 0:
        return 0
    return i + 1 if i % 2 == 1 else i - 1


def collide(f):
    keep = 1.0 - RELAX
    d = {i: f[i] - f[i + 1] for i in range(1, NQ, 2)}
    s = [f[i] + f[i + 1] for i in range(1, NQ, 2)]
    rho = ((s[0] + s[1]) + (s[2] + s[3])) + ((s[4] + s[5]) + (s[6] + s[7])) + (s[8] + f[0])
    mx = (d[1] + d[7]) + (d[9] + d[11]) + d[13]
    my = (d[3] + d[7]) + (d[15] - d[9]) + d[17]
    mz = (d[5] + d[11]) + (d[15] - d[13]) - d[17]
    inv = 1.0 / rho
    ux, uy, uz = mx * inv, my * inv, mz * inv
    a, b, c = mx * ux, my * uy, mz * uz
    base = rho - 1.5 * ((a + b) + c)
    w0, w1, w2 = RELAX / 3.0, RELAX / 18.0, RELAX / 36.0
    post = [None] * NQ
    post[0] = keep * f[0] + w0 * base
    one, two = w1 * base, w2 * base

    def pair(i, even, odd):
        post[i] = keep * f[i] + (even + odd)
        post[i + 1] = keep * f[i + 1] + (even - odd)

    k1, o1 = 4.5 * w1, 3.0 * w1
    pair(1, one + k1 * a, o1 * mx)
    pair(3, one + k1 * b, o1 * my)
    pair(5, one + k1 * c, o1 * mz)
    k2, o2 = 4.5 * w2, 3.0 * w2
    qx, qy, qz = o2 * mx, o2 * my, o2 * mz
    ka, kb, kc = k2 * a, k2 * b, k2 * c
    kx, ky = (2.0 * k2) * mx, (2.0 * k2) * my
    for i, even, cross, p, q in (
        (7, two + (ka + kb), kx * uy, qx, qy),
        (11, two + (ka + kc), kx * uz, qx, qz),
        (15, two + (kb + kc), ky * uz, qy, qz),
    ):
        pair(i, even + cross, p + q)
        pair(i + 2, even - cross, p - q)
    return post


def send_faces(x, t, last_x, last_t, raw, xp, xm, yp, ym):
    fixed = isinstance(x, int)
    rows = pl.ds(8 * t, 8)
    if fixed and x == last_x:
        for k, v in enumerate(raw(XP)):
            xp[k, rows, :] = v
    if fixed and x == 0:
        for k, v in enumerate(raw(XM)):
            xm[k, rows, :] = v
    for side, ref, group, row in ((last_t, yp, YP, 7), (0, ym, YM, 0)):
        if t != side:
            continue
        steps = [VEL[i][0] for i in group] + list(FLAG_X)
        for k, v in enumerate(raw(group)):
            to = x + steps[k]
            if fixed and not 0 <= to <= last_x:
                continue
            ref[k, pl.ds(to, 1), :] = v[row:row + 1]


def even(axis):
    return lax.axis_index(axis) % 2 == 0


def by_edge(axis, up, down):
    first = even(axis)
    return jnp.where(first, up, down), jnp.where(first, down, up)


def inner_columns(nx, body):
    def step(x, carry):
        body(x)
        return carry

    lax.fori_loop(1, nx - 1, step, 0)


def order_faces(xp, xm, x0, x1):
    for k in range(x0.shape[0]):
        x0[k], x1[k] = by_edge("gx", xp[k], xm[k])


def begin(x, t, f, solid, post, faces):
    nx, tiles = post.shape[1], post.shape[2] // 8
    rows = pl.ds(8 * t, 8)
    new = collide(f)
    flag = solid[x, rows, :].astype(jnp.float32)
    blocked = flag > 0.5
    for i in range(NQ):
        post[i, x, rows, :] = jnp.where(blocked, f[i] * MARK, new[i])

    def raw(group):
        return [new[i] for i in group] + [flag] * (3 if group in (YP, YM) else 1)

    send_faces(x, t, nx - 1, tiles - 1, raw, *faces)


def first_edge_kernel(f_hbm, solid_hbm, post, x0, x1, yp, ym, xp, xm, solid, sem):
    nx, ny = post.shape[1], post.shape[2]
    copies = []
    for n, x in enumerate((0, nx - 1)):
        at = pl.ds(x, 1)
        copies.append(pltpu.make_async_copy(solid_hbm.at[at], solid.at[at], sem.at[n]))
        copies.append(pltpu.make_async_copy(f_hbm.at[:, at], post.at[:, at], sem.at[2 + n]))
    for copy in copies:
        copy.start()
    for n, x in enumerate((0, nx - 1)):
        copies[2 * n].wait()
        copies[2 * n + 1].wait()
        for t in range(ny // 8):
            f = [post[i, x, pl.ds(8 * t, 8), :] for i in range(NQ)]
            begin(x, t, f, solid, post, (xp, xm, yp, ym))
    order_faces(xp, xm, x0, x1)


def first_inner_kernel(f_ref, solid, post_in, yp_in, ym_in, post, yp, ym):
    nx, ny = post.shape[1], post.shape[2]

    def body(x):
        for t in range(ny // 8):
            f = [f_ref[i, x, pl.ds(8 * t, 8), :] for i in range(NQ)]
            begin(x, t, f, solid, post, (None, None, yp, ym))

    inner_columns(nx, body)


def corner_kernel(yp, ym, r0, r1, y0, y1):
    nx, ny = yp.shape[1], r0.shape[1]
    row = lax.broadcasted_iota(jnp.int32, yp.shape[1:], 0)

    def filled(ref, k, group, end):
        step = VEL[group[k]][0] if k < 5 else FLAG_X[k - 5]
        cz = VEL[group[k]][2] if k < 5 else 0
        v = ref[k]
        if step == 0 or cz:
            return v
        side = XP if step == 1 else XM
        at = side.index(group[k]) if k < 5 else 5
        right, left = by_edge("gx", r0[at, end:end + 1], r1[at, end:end + 1])
        return jnp.where(row == (0 if step == 1 else nx - 1), left if step == 1 else right, v)

    for k in range(yp.shape[0]):
        y0[k], y1[k] = by_edge("gy", filled(yp, k, YP, ny - 1), filled(ym, k, YM, 0))


def mark_halos(r0, r1, s0, s1, flag_x0, flag_x1, flag_y0, flag_y1, hx, hy):
    flags = by_edge("gx", flag_x0[5], flag_x1[5])
    for k in range(5):
        values = by_edge("gx", r0[k], r1[k])
        for side in range(2):
            hx[side, k] = jnp.where(flags[1 - side] > 0.5, MARK, values[1 - side])
    for k in range(5):
        values = by_edge("gy", s0[k], s1[k])
        for side, group in enumerate((YP, YM)):
            plane = 5 + FLAG_X.index(VEL[group[k]][0])
            flag = by_edge("gy", flag_y0[plane], flag_y1[plane])[1 - side]
            hy[side, k] = jnp.where(flag > 0.5, MARK, values[1 - side])


def stream(post, hx, hy, x, t):
    nx, tiles = post.shape[1], post.shape[2] // 8
    fixed = isinstance(x, int)
    own = [post[i, x, pl.ds(8 * t, 8), :] for i in range(NQ)]
    row = lax.broadcasted_iota(jnp.int32, (8, 128), 0)
    f = [own[0]]
    for i in range(1, NQ):
        cx, cy, cz = VEL[i]
        if fixed and not 0 <= x - cx < nx:
            view = hx.at[0, XP.index(i)] if cx == 1 else hx.at[1, XM.index(i)]
        else:
            view = post.at[i, x - cx]
        if cy == 1 and t == 0:
            halo = jnp.broadcast_to(hy[0, YP.index(i), pl.ds(x, 1), :], (8, 128))
            v = jnp.where(row == 0, halo, pltpu.roll(view[pl.ds(0, 8), :], 1, 0))
        elif cy == -1 and t == tiles - 1:
            halo = jnp.broadcast_to(hy[1, YM.index(i), pl.ds(x, 1), :], (8, 128))
            v = jnp.where(row == 7, halo, pltpu.roll(view[pl.ds(8 * t, 8), :], 7, 0))
        else:
            v = view[pl.ds(8 * t - cy, 8), :]
        if cz:
            v = pltpu.roll(v, cz % 128, 1)
        f.append(jnp.where(v < EDGE, own[opposite(i)], v))
    return f, own, own[0] > EDGE


def advance(post, hx, hy, x, t, out, faces):
    nx, tiles = post.shape[1], post.shape[2] // 8
    f, own, fluid = stream(post, hx, hy, x, t)
    new = collide(f)
    for i in range(NQ):
        out[i, x, pl.ds(8 * t, 8), :] = jnp.where(fluid, new[i], own[i])
    send_faces(x, t, nx - 1, tiles - 1, lambda group: [new[i] for i in group], *faces)


def centre_kernel(post, out):
    def body(x):
        for t in range(1, post.shape[2] // 8 - 1):
            advance(post, None, None, x, t, out, (None,) * 4)

    inner_columns(post.shape[1], body)


def edge_kernel(post, *refs):
    halos, (out_in, out, x0, x1, yp, ym, hy, xp, xm, hx) = refs[:8], refs[8:]
    nx, ny = post.shape[1], post.shape[2]
    mark_halos(*halos, hx, hy)
    for x in (0, nx - 1):
        for t in range(ny // 8):
            advance(post, hx, hy, x, t, out, (xp, xm, yp, ym))
    order_faces(xp, xm, x0, x1)


def rim_kernel(post, hy, out_in, yp_in, ym_in, out, yp, ym):
    def body(x):
        for t in (0, post.shape[2] // 8 - 1):
            advance(post, None, hy, x, t, out, (None, None, yp, ym))

    inner_columns(post.shape[1], body)


def finish(post, hx, hy, x, t, stage):
    f, own, fluid = stream(post, hx, hy, x, t)
    for i in range(NQ):
        stage[i, x, pl.ds(8 * t, 8), :] = jnp.where(fluid, f[i], own[i] * (1.0 / MARK))


def send_out(stage, out_hbm, sem, x, nx, y, ny):
    copy = pltpu.make_async_copy(
        stage.at[:, pl.ds(x, nx), pl.ds(y, ny)], out_hbm.at[:, pl.ds(x, nx), pl.ds(y, ny)], sem
    )
    copy.start()
    return copy


def last_centre_kernel(post, out_hbm, stage, sem):
    nx, ny = post.shape[1], post.shape[2]
    parts = sem.shape[0]
    size = (nx - 2) // parts
    copies = []
    for p in range(parts):

        def step(x, carry):
            for t in range(1, ny // 8 - 1):
                finish(post, None, None, x, t, stage)
            return carry

        low = 1 + p * size
        lax.fori_loop(low, low + size, step, 0)
        copies.append(send_out(stage, out_hbm, sem.at[p], low, size, 8, ny - 16))
    for copy in copies:
        copy.wait()


def last_kernel(post, *refs):
    halos, (out_in, out_hbm, stage, hx, hy, sem) = refs[:8], refs[8:]
    nx, ny = post.shape[1], post.shape[2]
    mark_halos(*halos, hx, hy)
    copies = []
    for n, x in enumerate((0, nx - 1)):
        for t in range(ny // 8):
            finish(post, hx, hy, x, t, stage)
        copies.append(send_out(stage, out_hbm, sem.at[n], x, 1, 0, ny))
    parts = (sem.shape[0] - 2) // 2
    size = (nx - 2) // parts
    for p in range(parts):

        def step(x, carry):
            for t in (0, ny // 8 - 1):
                finish(post, None, hy, x, t, stage)
            return carry

        low = 1 + p * size
        lax.fori_loop(low, low + size, step, 0)
        for n, y in enumerate((0, ny - 8)):
            copies.append(send_out(stage, out_hbm, sem.at[2 + 2 * p + n], low, size, y, 8))
    for copy in copies:
        copy.wait()


def swap(value, axis, edge):
    count = lax.axis_size(axis)
    pairs = [((2 * j + edge) % count, (2 * j + edge + 1) % count) for j in range(count // 2)]
    return lax.ppermute(value, axis, pairs + [(b, a) for a, b in pairs])


def local(populations, solid):
    _, nx, ny, nz = populations.shape
    f32 = jnp.float32
    anywhere = pl.BlockSpec(memory_space=pl.ANY)
    onchip = pl.BlockSpec(memory_space=pltpu.VMEM)
    state = pltpu.VMEM(populations.shape, f32)
    params = pltpu.CompilerParams(vmem_limit_bytes=24 << 20)

    def kernel(body, name, out_shape, in_specs, out_specs=None, scratch=(), aliases={}):
        return pl.pallas_call(
            body,
            out_shape=out_shape,
            in_specs=in_specs,
            out_specs=out_specs or (onchip,) * len(out_shape),
            scratch_shapes=list(scratch),
            input_output_aliases=aliases,
            compiler_params=params,
            cost_estimate=pl.CostEstimate(flops=1 << 24, bytes_accessed=1 << 22, transcendentals=0),
            name=name,
        )

    def held(value):
        return pltpu.with_memory_space_constraint(value, pltpu.VMEM)

    def face_x(planes):
        return jax.ShapeDtypeStruct((planes, ny, nz), f32)

    def face_y(planes):
        return jax.ShapeDtypeStruct((planes, nx, nz), f32)

    def swap_x(x0, x1):
        return swap(x0, "gx", 0), swap(x1, "gx", 1)

    def swap_y(yp, ym, r0, r1):
        shape = jax.ShapeDtypeStruct(yp.shape, f32)
        y0, y1 = kernel(corner_kernel, "corners", (shape,) * 2, [onchip] * 4)(yp, ym, r0, r1)
        return swap(y0, "gy", 0), swap(y1, "gy", 1)

    post, x0, x1, yp, ym = kernel(
        first_edge_kernel,
        "first_edge",
        (state, face_x(6), face_x(6), face_y(8), face_y(8)),
        [anywhere] * 2,
        scratch=[pltpu.VMEM((6, ny, nz), f32)] * 2
        + [pltpu.VMEM(solid.shape, jnp.int32), pltpu.SemaphoreType.DMA((4,))],
    )(
        pltpu.with_memory_space_constraint(populations, pltpu.HBM),
        pltpu.with_memory_space_constraint(solid, pltpu.HBM),
    )
    r0, r1 = swap_x(x0, x1)
    post, yp, ym = kernel(
        first_inner_kernel,
        "first_inner",
        (state, face_y(8), face_y(8)),
        [onchip] * 5,
        aliases={2: 0, 3: 1, 4: 2},
    )(held(populations), held(solid), held(post), yp, ym)
    halos = flags = (r0, r1, *swap_y(yp, ym, r0, r1))
    marked = [pltpu.VMEM((2, 5, ny, nz), f32), pltpu.VMEM((2, 5, nx, nz), f32)]
    for _ in range(ITERS - 1):
        post = held(post)
        (new,) = kernel(centre_kernel, "centre", (state,), [onchip])(post)
        new, x0, x1, yp, ym, hy = kernel(
            edge_kernel,
            "edge",
            (state, face_x(5), face_x(5), face_y(5), face_y(5), jax.ShapeDtypeStruct((2, 5, nx, nz), f32)),
            [onchip] * 10,
            scratch=[pltpu.VMEM((5, ny, nz), f32)] * 2 + marked[:1],
            aliases={9: 0},
        )(post, *halos, *flags, held(new))
        r0, r1 = swap_x(x0, x1)
        new, yp, ym = kernel(
            rim_kernel,
            "rim",
            (state, face_y(5), face_y(5)),
            [onchip] * 5,
            aliases={2: 0, 3: 1, 4: 2},
        )(post, hy, held(new), yp, ym)
        halos = (r0, r1, *swap_y(yp, ym, r0, r1))
        post = new
    post = held(post)
    whole = jax.ShapeDtypeStruct(populations.shape, f32)
    stage = pltpu.VMEM(populations.shape, f32)
    (out,) = kernel(
        last_centre_kernel, "last_centre", (whole,), [onchip], (anywhere,),
        scratch=[stage, pltpu.SemaphoreType.DMA((2,))],
    )(post)
    (out,) = kernel(
        last_kernel, "last", (whole,), [onchip] * 9 + [anywhere], (anywhere,),
        scratch=[stage] + marked + [pltpu.SemaphoreType.DMA((6,))],
        aliases={9: 0},
    )(post, *halos, *flags, out)
    return out


def solution(mesh):
    in_specs = (P(None, "gx", "gy", None), P("gx", "gy", None))
    out_specs = P(None, "gx", "gy", None)
    return jax.shard_map(local, mesh=mesh, in_specs=in_specs, out_specs=out_specs, check_vma=False)
```

```python
import jax
import jax.numpy as jnp
from jax import lax
from jax.experimental import pallas as pl
from jax.experimental.pallas import tpu as pltpu
from jax.sharding import PartitionSpec as P


ITERS = 3
NQ = 19
VEL = (
    (0, 0, 0),
    (1, 0, 0), (-1, 0, 0), (0, 1, 0), (0, -1, 0), (0, 0, 1), (0, 0, -1),
    (1, 1, 0), (-1, -1, 0), (1, -1, 0), (-1, 1, 0),
    (1, 0, 1), (-1, 0, -1), (1, 0, -1), (-1, 0, 1),
    (0, 1, 1), (0, -1, -1), (0, 1, -1), (0, -1, 1),
)
RELAX = 1.6
XP = tuple(i for i in range(NQ) if VEL[i][0] == 1)
XM = tuple(i for i in range(NQ) if VEL[i][0] == -1)
YP = tuple(i for i in range(NQ) if VEL[i][1] == 1)
YM = tuple(i for i in range(NQ) if VEL[i][1] == -1)
MARK = -float(2 ** 20)
EDGE = -1e5


def opposite(i):
    if i == 0:
        return 0
    return i + 1 if i % 2 == 1 else i - 1


def collide(f):
    keep = 1.0 - RELAX
    d = {i: f[i] - f[i + 1] for i in range(1, NQ, 2)}
    s = [f[i] + f[i + 1] for i in range(1, NQ, 2)]
    rho = ((s[0] + s[1]) + (s[2] + s[3])) + ((s[4] + s[5]) + (s[6] + s[7])) + (s[8] + f[0])
    mx = (d[1] + d[7]) + (d[9] + d[11]) + d[13]
    my = (d[3] + d[7]) + (d[15] - d[9]) + d[17]
    mz = (d[5] + d[11]) + (d[15] - d[13]) - d[17]
    inv = 1.0 / rho
    ux, uy, uz = mx * inv, my * inv, mz * inv
    a, b, c = mx * ux, my * uy, mz * uz
    base = rho - 1.5 * ((a + b) + c)
    w0, w1, w2 = RELAX / 3.0, RELAX / 18.0, RELAX / 36.0
    post = [None] * NQ
    post[0] = keep * f[0] + w0 * base
    one, two = w1 * base, w2 * base

    def pair(i, even, odd):
        post[i] = keep * f[i] + (even + odd)
        post[i + 1] = keep * f[i + 1] + (even - odd)

    k1, o1 = 4.5 * w1, 3.0 * w1
    pair(1, one + k1 * a, o1 * mx)
    pair(3, one + k1 * b, o1 * my)
    pair(5, one + k1 * c, o1 * mz)
    k2, o2 = 4.5 * w2, 3.0 * w2
    qx, qy, qz = o2 * mx, o2 * my, o2 * mz
    ka, kb, kc = k2 * a, k2 * b, k2 * c
    kx, ky = (2.0 * k2) * mx, (2.0 * k2) * my
    for i, even, cross, p, q in (
        (7, two + (ka + kb), kx * uy, qx, qy),
        (11, two + (ka + kc), kx * uz, qx, qz),
        (15, two + (kb + kc), ky * uz, qy, qz),
    ):
        pair(i, even + cross, p + q)
        pair(i + 2, even - cross, p - q)
    return post


def send_faces(x, t, last_x, last_t, raw, xp, xm, yp, ym):
    fixed = isinstance(x, int)
    rows = pl.ds(8 * t, 8)
    if fixed and x == last_x:
        for k, v in enumerate(raw(XP)):
            xp[k, rows, :] = v
    if fixed and x == 0:
        for k, v in enumerate(raw(XM)):
            xm[k, rows, :] = v
    for side, ref, group, row in ((last_t, yp, YP, 7), (0, ym, YM, 0)):
        if t != side:
            continue
        steps = [VEL[i][0] for i in group] + [0]
        for k, v in enumerate(raw(group)):
            to = x + steps[k]
            if fixed and not 0 <= to <= last_x:
                continue
            ref[k, pl.ds(to, 1), :] = v[row:row + 1]


def even(axis):
    return lax.axis_index(axis) % 2 == 0


def by_edge(axis, up, down):
    first = even(axis)
    return jnp.where(first, up, down), jnp.where(first, down, up)


def inner_columns(nx, body):
    def step(x, carry):
        body(x)
        return carry

    lax.fori_loop(1, nx - 1, step, 0)


def order_faces(xp, xm, x0, x1):
    for k in range(x0.shape[0]):
        x0[k], x1[k] = by_edge("gx", xp[k], xm[k])


def begin(x, t, f, solid, post, faces):
    nx, tiles = post.shape[1], post.shape[2] // 8
    rows = pl.ds(8 * t, 8)
    new = collide(f)
    flag = solid[x, rows, :].astype(jnp.float32)
    blocked = flag > 0.5
    for i in range(NQ):
        post[i, x, rows, :] = jnp.where(blocked, f[i] * MARK, new[i])

    def raw(group):
        return [new[i] for i in group] + [flag]

    send_faces(x, t, nx - 1, tiles - 1, raw, *faces)


def first_edge_kernel(f_hbm, solid_hbm, post, x0, x1, yp, ym, xp, xm, solid, sem):
    nx, ny = post.shape[1], post.shape[2]
    copies = []
    for n, x in enumerate((0, nx - 1)):
        at = pl.ds(x, 1)
        copies.append(pltpu.make_async_copy(solid_hbm.at[at], solid.at[at], sem.at[n]))
        copies.append(pltpu.make_async_copy(f_hbm.at[:, at], post.at[:, at], sem.at[2 + n]))
    for copy in copies:
        copy.start()
    for n, x in enumerate((0, nx - 1)):
        copies[2 * n].wait()
        copies[2 * n + 1].wait()
        for t in range(ny // 8):
            f = [post[i, x, pl.ds(8 * t, 8), :] for i in range(NQ)]
            begin(x, t, f, solid, post, (xp, xm, yp, ym))
    order_faces(xp, xm, x0, x1)


def first_inner_kernel(f_ref, solid, post_in, yp_in, ym_in, post, yp, ym):
    nx, ny = post.shape[1], post.shape[2]

    def body(x):
        for t in range(ny // 8):
            f = [f_ref[i, x, pl.ds(8 * t, 8), :] for i in range(NQ)]
            begin(x, t, f, solid, post, (None, None, yp, ym))

    inner_columns(nx, body)


def corner_kernel(yp, ym, r0, r1, y0, y1):
    planes, nx, _ = yp.shape
    ny = r0.shape[1]
    row = lax.broadcasted_iota(jnp.int32, yp.shape[1:], 0)

    def filled(ref, k, group, end):
        step, _, cz = VEL[group[k]]
        if step == 0 or cz:
            return ref[k]
        at = (XP if step == 1 else XM).index(group[k])
        right, left = by_edge("gx", r0[at, end:end + 1], r1[at, end:end + 1])
        return jnp.where(row == (0 if step == 1 else nx - 1), left if step == 1 else right, ref[k])

    for k in range(5):
        y0[pl.ds(k * nx, nx)], y1[pl.ds(k * nx, nx)] = by_edge(
            "gy", filled(yp, k, YP, ny - 1), filled(ym, k, YM, 0)
        )
    if planes > 5:
        y0[pl.ds(5 * nx, nx)], y1[pl.ds(5 * nx, nx)] = by_edge("gy", yp[5], ym[5])
        up = by_edge("gx", r0[5, ny - 1:ny], r1[5, ny - 1:ny])
        down = by_edge("gx", r0[5, 0:1], r1[5, 0:1])
        for n in range(2):
            at = pl.ds(6 * nx + n, 1)
            y0[at], y1[at] = by_edge("gy", up[1 - n], down[1 - n])
        rest = pl.ds(6 * nx + 2, 6)
        y0[rest] = y1[rest] = jnp.zeros((6, 128), jnp.float32)


def mark_x(r0, r1, flag_x0, flag_x1, hx):
    flags = by_edge("gx", flag_x0[5], flag_x1[5])
    for k in range(5):
        values = by_edge("gx", r0[k], r1[k])
        for side in range(2):
            hx[side, k] = jnp.where(flags[1 - side] > 0.5, MARK, values[1 - side])


def mark_y(s0, s1, flag_y0, flag_y1, hy):
    nx = hy.shape[2]
    row = lax.broadcasted_iota(jnp.int32, hy.shape[2:], 0)
    own = by_edge("gy", flag_y0[pl.ds(5 * nx, nx)], flag_y1[pl.ds(5 * nx, nx)])
    left, right = [
        by_edge("gy", flag_y0[pl.ds(6 * nx + n, 1)], flag_y1[pl.ds(6 * nx + n, 1)]) for n in range(2)
    ]
    for side, group in enumerate((YP, YM)):
        flags = {
            0: own[1 - side],
            1: jnp.where(row == 0, left[1 - side], pltpu.roll(own[1 - side], 1, 0)),
            -1: jnp.where(row == nx - 1, right[1 - side], pltpu.roll(own[1 - side], nx - 1, 0)),
        }
        for k in range(5):
            at = pl.ds(k * nx, nx)
            value = by_edge("gy", s0[at], s1[at])[1 - side]
            hy[side, k] = jnp.where(flags[VEL[group[k]][0]] > 0.5, MARK, value)


def arriving(post, hx, hy, x, t, i):
    nx, tiles = post.shape[1], post.shape[2] // 8
    cx, cy, cz = VEL[i]
    if isinstance(x, int) and not 0 <= x - cx < nx:
        view = hx.at[0, XP.index(i)] if cx == 1 else hx.at[1, XM.index(i)]
    else:
        view = post.at[i, x - cx]
    row = lax.broadcasted_iota(jnp.int32, (8, 128), 0)
    if cy == 1 and t == 0:
        v = pltpu.roll(view[pl.ds(0, 8), :], 1, 0)
        if hy is not None:
            v = jnp.where(row == 0, jnp.broadcast_to(hy[0, YP.index(i), pl.ds(x, 1), :], (8, 128)), v)
    elif cy == -1 and t == tiles - 1:
        v = pltpu.roll(view[pl.ds(8 * t, 8), :], 7, 0)
        if hy is not None:
            v = jnp.where(row == 7, jnp.broadcast_to(hy[1, YM.index(i), pl.ds(x, 1), :], (8, 128)), v)
    else:
        v = view[pl.ds(8 * t - cy, 8), :]
    return pltpu.roll(v, cz % 128, 1) if cz else v


def stream(post, hx, hy, x, t):
    own = [post[i, x, pl.ds(8 * t, 8), :] for i in range(NQ)]
    f = [own[0]]
    for i in range(1, NQ):
        v = arriving(post, hx, hy, x, t, i)
        f.append(jnp.where(v < EDGE, own[opposite(i)], v))
    return f, own, own[0] > EDGE


def advance(post, hx, hy, x, t, out, faces):
    nx, tiles = post.shape[1], post.shape[2] // 8
    f, own, fluid = stream(post, hx, hy, x, t)
    new = collide(f)
    for i in range(NQ):
        out[i, x, pl.ds(8 * t, 8), :] = jnp.where(fluid, new[i], own[i])
    send_faces(x, t, nx - 1, tiles - 1, lambda group: [new[i] for i in group], *faces)


def centre_kernel(post, r0, r1, flag_x0, flag_x1, out, xp, xm, hx):
    nx, ny = post.shape[1], post.shape[2]
    mark_x(r0, r1, flag_x0, flag_x1, hx)

    def body(x):
        for t in range(1, ny // 8 - 1):
            advance(post, hx, None, x, t, out, (xp, xm, None, None))

    body(0)
    body(nx - 1)
    inner_columns(nx, body)


def edge_kernel(post, hx, xp_in, xm_in, s0, s1, flag_y0, flag_y1, out_in, out, x0, x1, yp, ym, hy, xp, xm):
    nx, ny = post.shape[1], post.shape[2]
    mark_y(s0, s1, flag_y0, flag_y1, hy)
    for x in (0, nx - 1):
        for t in (0, ny // 8 - 1):
            advance(post, hx, hy, x, t, out, (xp, xm, yp, ym))
    for rows, up, down in (
        (pl.ds(0, 8), xp, xm),
        (pl.ds(8, ny - 16), xp_in, xm_in),
        (pl.ds(ny - 8, 8), xp, xm),
    ):
        for k in range(5):
            x0[k, rows, :], x1[k, rows, :] = by_edge("gx", up[k, rows, :], down[k, rows, :])


def rim_kernel(post, hy, out_in, yp_in, ym_in, out, yp, ym):
    def body(x):
        for t in (0, post.shape[2] // 8 - 1):
            advance(post, None, hy, x, t, out, (None, None, yp, ym))

    inner_columns(post.shape[1], body)


def last_centre_kernel(post, r0, r1, flag_x0, flag_x1, out_hbm, hx, stage, sem):
    nx, ny = post.shape[1], post.shape[2]
    mark_x(r0, r1, flag_x0, flag_x1, hx)

    def body(x):
        for t in range(ny // 8):
            f, own, fluid = stream(post, hx, None, x, t)
            for i in range(NQ):
                stage[i, x, pl.ds(8 * t, 8), :] = jnp.where(fluid, f[i], own[i] * (1.0 / MARK))

    def step(x, carry):
        body(x)
        return carry

    parts = sem.shape[0]
    size = nx // parts
    copies = []
    for p in range(parts):
        low, high = p * size, (p + 1) * size
        if p == 0:
            body(0)
        lax.fori_loop(max(low, 1), min(high, nx - 1), step, 0)
        if p == parts - 1:
            body(nx - 1)
        at = pl.ds(low, size)
        copies.append(pltpu.make_async_copy(stage.at[:, at], out_hbm.at[:, at], sem.at[p]))
        copies[-1].start()
    for copy in copies:
        copy.wait()


def last_kernel(post, hx, s0, s1, flag_y0, flag_y1, out_in, out_hbm, stage, hy, sem):
    nx, ny = post.shape[1], post.shape[2]
    mark_y(s0, s1, flag_y0, flag_y1, hy)
    copies = []
    for side, (t, group) in enumerate(((0, YP), (ny // 8 - 1, YM))):
        rows = pl.ds(8 * t, 8)
        fluid = [post[0, x, rows, :] > EDGE for x in range(nx)]
        for k, i in enumerate(group):
            for x in range(nx):
                v = arriving(post, hx, hy, x, t, i)
                v = jnp.where(v < EDGE, post[opposite(i), x, rows, :], v)
                stage[side, k, x] = jnp.where(fluid[x], v, post[i, x, rows, :] * (1.0 / MARK))
            copies.append(pltpu.make_async_copy(stage.at[side, k], out_hbm.at[i, :, rows], sem.at[side, k]))
            copies[-1].start()
    for copy in copies:
        copy.wait()


def swap(value, axis, edge):
    count = lax.axis_size(axis)
    pairs = [((2 * j + edge) % count, (2 * j + edge + 1) % count) for j in range(count // 2)]
    return lax.ppermute(value, axis, pairs + [(b, a) for a, b in pairs])


def local(populations, solid):
    _, nx, ny, nz = populations.shape
    f32 = jnp.float32
    anywhere = pl.BlockSpec(memory_space=pl.ANY)
    onchip = pl.BlockSpec(memory_space=pltpu.VMEM)
    state = pltpu.VMEM(populations.shape, f32)
    params = pltpu.CompilerParams(vmem_limit_bytes=24 << 20)

    def kernel(body, out_shape, in_specs, out_specs=None, scratch=(), aliases={}):
        return pl.pallas_call(
            body,
            out_shape=out_shape,
            in_specs=in_specs,
            out_specs=out_specs or (onchip,) * len(out_shape),
            scratch_shapes=list(scratch),
            input_output_aliases=aliases,
            compiler_params=params,
            cost_estimate=pl.CostEstimate(flops=1 << 24, bytes_accessed=1 << 22, transcendentals=0),
        )

    def held(value):
        return pltpu.with_memory_space_constraint(value, pltpu.VMEM)

    def face_x(planes):
        return jax.ShapeDtypeStruct((planes, ny, nz), f32)

    def face_y(planes):
        return jax.ShapeDtypeStruct((planes, nx, nz), f32)

    def swap_x(x0, x1):
        return swap(x0, "gx", 0), swap(x1, "gx", 1)

    def swap_y(yp, ym, r0, r1):
        rows = 5 * nx if yp.shape[0] == 5 else 6 * nx + 8
        shape = jax.ShapeDtypeStruct((rows, nz), f32)
        y0, y1 = kernel(corner_kernel, (shape,) * 2, [onchip] * 4)(yp, ym, r0, r1)
        return swap(y0, "gy", 0), swap(y1, "gy", 1)

    post, x0, x1, yp, ym = kernel(
        first_edge_kernel,
        (state, face_x(6), face_x(6), face_y(6), face_y(6)),
        [anywhere] * 2,
        scratch=[pltpu.VMEM((6, ny, nz), f32)] * 2
        + [pltpu.VMEM(solid.shape, jnp.int32), pltpu.SemaphoreType.DMA((4,))],
    )(
        pltpu.with_memory_space_constraint(populations, pltpu.HBM),
        pltpu.with_memory_space_constraint(solid, pltpu.HBM),
    )
    r0, r1 = swap_x(x0, x1)
    post, yp, ym = kernel(
        first_inner_kernel, (state, face_y(6), face_y(6)), [onchip] * 5, aliases={2: 0, 3: 1, 4: 2}
    )(held(populations), held(solid), held(post), yp, ym)
    flag_x = (r0, r1)
    s0, s1 = flag_y = swap_y(yp, ym, r0, r1)
    marked_x = jax.ShapeDtypeStruct((2, 5, ny, nz), f32)
    marked_y = jax.ShapeDtypeStruct((2, 5, nx, nz), f32)
    for _ in range(1, ITERS):
        post = held(post)
        new, xp, xm, hx = kernel(
            centre_kernel, (state, face_x(5), face_x(5), marked_x), [onchip] * 5
        )(post, r0, r1, *flag_x)
        new, x0, x1, yp, ym, hy = kernel(
            edge_kernel,
            (state, face_x(5), face_x(5), face_y(5), face_y(5), marked_y),
            [onchip] * 9,
            scratch=[pltpu.VMEM((5, ny, nz), f32)] * 2,
            aliases={8: 0},
        )(post, hx, xp, xm, s0, s1, *flag_y, held(new))
        r0, r1 = swap_x(x0, x1)
        new, yp, ym = kernel(
            rim_kernel, (state, face_y(5), face_y(5)), [onchip] * 5, aliases={2: 0, 3: 1, 4: 2}
        )(post, hy, held(new), yp, ym)
        s0, s1 = swap_y(yp, ym, r0, r1)
        post = new
    post = held(post)
    whole = jax.ShapeDtypeStruct(populations.shape, f32)
    out, hx = kernel(
        last_centre_kernel,
        (whole, marked_x),
        [onchip] * 5,
        (anywhere, onchip),
        scratch=[pltpu.VMEM(populations.shape, f32), pltpu.SemaphoreType.DMA((4,))],
    )(post, r0, r1, *flag_x)
    (out,) = kernel(
        last_kernel,
        (whole,),
        [onchip] * 6 + [anywhere],
        (anywhere,),
        scratch=[
            pltpu.VMEM((2, 5, nx, 8, nz), f32),
            pltpu.VMEM((2, 5, nx, nz), f32),
            pltpu.SemaphoreType.DMA((2, 5)),
        ],
        aliases={6: 0},
    )(post, hx, s0, s1, *flag_y, out)
    return out


def solution(mesh):
    in_specs = (P(None, "gx", "gy", None), P("gx", "gy", None))
    out_specs = P(None, "gx", "gy", None)
    return jax.shard_map(local, mesh=mesh, in_specs=in_specs, out_specs=out_specs, check_vma=False)
```

```python
import jax
import jax.numpy as jnp
from jax import lax
from jax.experimental import pallas as pl
from jax.experimental.pallas import tpu as pltpu
from jax.sharding import PartitionSpec as P


ITERS = 3
NQ = 19
VEL = (
    (0, 0, 0),
    (1, 0, 0), (-1, 0, 0), (0, 1, 0), (0, -1, 0), (0, 0, 1), (0, 0, -1),
    (1, 1, 0), (-1, -1, 0), (1, -1, 0), (-1, 1, 0),
    (1, 0, 1), (-1, 0, -1), (1, 0, -1), (-1, 0, 1),
    (0, 1, 1), (0, -1, -1), (0, 1, -1), (0, -1, 1),
)
RELAX = 1.6
XP = tuple(i for i in range(NQ) if VEL[i][0] == 1)
XM = tuple(i for i in range(NQ) if VEL[i][0] == -1)
YP = tuple(i for i in range(NQ) if VEL[i][1] == 1)
YM = tuple(i for i in range(NQ) if VEL[i][1] == -1)
MARK = -float(2 ** 20)
EDGE = -1e5


def opposite(i):
    if i == 0:
        return 0
    return i + 1 if i % 2 == 1 else i - 1


def collide(f):
    keep = 1.0 - RELAX
    d = {i: f[i] - f[i + 1] for i in range(1, NQ, 2)}
    s = [f[i] + f[i + 1] for i in range(1, NQ, 2)]
    rho = ((s[0] + s[1]) + (s[2] + s[3])) + ((s[4] + s[5]) + (s[6] + s[7])) + (s[8] + f[0])
    mx = (d[1] + d[7]) + (d[9] + d[11]) + d[13]
    my = (d[3] + d[7]) + (d[15] - d[9]) + d[17]
    mz = (d[5] + d[11]) + (d[15] - d[13]) - d[17]
    inv = 1.0 / rho
    ux, uy, uz = mx * inv, my * inv, mz * inv
    a, b, c = mx * ux, my * uy, mz * uz
    base = rho - 1.5 * ((a + b) + c)
    w0, w1, w2 = RELAX / 3.0, RELAX / 18.0, RELAX / 36.0
    post = [None] * NQ
    post[0] = keep * f[0] + w0 * base
    one, two = w1 * base, w2 * base

    def pair(i, even, odd):
        post[i] = keep * f[i] + (even + odd)
        post[i + 1] = keep * f[i + 1] + (even - odd)

    k1, o1 = 4.5 * w1, 3.0 * w1
    pair(1, one + k1 * a, o1 * mx)
    pair(3, one + k1 * b, o1 * my)
    pair(5, one + k1 * c, o1 * mz)
    k2, o2 = 4.5 * w2, 3.0 * w2
    qx, qy, qz = o2 * mx, o2 * my, o2 * mz
    ka, kb, kc = k2 * a, k2 * b, k2 * c
    kx, ky = (2.0 * k2) * mx, (2.0 * k2) * my
    for i, even, cross, p, q in (
        (7, two + (ka + kb), kx * uy, qx, qy),
        (11, two + (ka + kc), kx * uz, qx, qz),
        (15, two + (kb + kc), ky * uz, qy, qz),
    ):
        pair(i, even + cross, p + q)
        pair(i + 2, even - cross, p - q)
    return post


def send_faces(x, t, last_x, last_t, raw, xp, xm, yp, ym):
    fixed = isinstance(x, int)
    rows = pl.ds(8 * t, 8)
    if fixed and x == last_x:
        for k, v in enumerate(raw(XP)):
            xp[k, rows, :] = v
    if fixed and x == 0:
        for k, v in enumerate(raw(XM)):
            xm[k, rows, :] = v
    for side, ref, group, row in ((last_t, yp, YP, 7), (0, ym, YM, 0)):
        if t != side:
            continue
        steps = [VEL[i][0] for i in group] + [0]
        for k, v in enumerate(raw(group)):
            to = x + steps[k]
            if fixed and not 0 <= to <= last_x:
                continue
            ref[k, pl.ds(to, 1), :] = v[row:row + 1]


def even(axis):
    return lax.axis_index(axis) % 2 == 0


def by_edge(axis, up, down):
    first = even(axis)
    return jnp.where(first, up, down), jnp.where(first, down, up)


def inner_columns(nx, body, unroll=1):
    def step(x, carry):
        body(x)
        return carry

    lax.fori_loop(1, nx - 1, step, 0, unroll=unroll)


def order_faces(xp, xm, x0, x1):
    for k in range(x0.shape[0]):
        x0[k], x1[k] = by_edge("gx", xp[k], xm[k])


def begin(x, t, f, solid, post, faces):
    nx, tiles = post.shape[1], post.shape[2] // 8
    rows = pl.ds(8 * t, 8)
    new = collide(f)
    flag = solid[x, rows, :].astype(jnp.float32)
    blocked = flag > 0.5
    for i in range(NQ):
        post[i, x, rows, :] = jnp.where(blocked, f[i] * MARK, new[i])

    def raw(group):
        return [new[i] for i in group] + [flag]

    send_faces(x, t, nx - 1, tiles - 1, raw, *faces)


def first_edge_kernel(f_hbm, solid_hbm, post, x0, x1, yp, ym, xp, xm, solid, sem):
    nx, ny = post.shape[1], post.shape[2]
    copies = []
    for n, x in enumerate((0, nx - 1)):
        at = pl.ds(x, 1)
        copies.append(pltpu.make_async_copy(solid_hbm.at[at], solid.at[at], sem.at[n]))
        copies.append(pltpu.make_async_copy(f_hbm.at[:, at], post.at[:, at], sem.at[2 + n]))
    for copy in copies:
        copy.start()
    for n, x in enumerate((0, nx - 1)):
        copies[2 * n].wait()
        copies[2 * n + 1].wait()
        for t in range(ny // 8):
            f = [post[i, x, pl.ds(8 * t, 8), :] for i in range(NQ)]
            begin(x, t, f, solid, post, (xp, xm, yp, ym))
    order_faces(xp, xm, x0, x1)


def first_inner_kernel(f_ref, solid, post_in, yp_in, ym_in, post, yp, ym):
    nx, ny = post.shape[1], post.shape[2]

    def body(x):
        for t in range(ny // 8):
            f = [f_ref[i, x, pl.ds(8 * t, 8), :] for i in range(NQ)]
            begin(x, t, f, solid, post, (None, None, yp, ym))

    inner_columns(nx, body)


def corner_kernel(yp, ym, r0, r1, y0, y1):
    planes, nx, _ = yp.shape
    ny = r0.shape[1]
    row = lax.broadcasted_iota(jnp.int32, yp.shape[1:], 0)

    def filled(ref, k, group, end):
        step, _, cz = VEL[group[k]]
        if step == 0 or cz:
            return ref[k]
        at = (XP if step == 1 else XM).index(group[k])
        right, left = by_edge("gx", r0[at, end:end + 1], r1[at, end:end + 1])
        return jnp.where(row == (0 if step == 1 else nx - 1), left if step == 1 else right, ref[k])

    for k in range(5):
        y0[pl.ds(k * nx, nx)], y1[pl.ds(k * nx, nx)] = by_edge(
            "gy", filled(yp, k, YP, ny - 1), filled(ym, k, YM, 0)
        )
    if planes > 5:
        y0[pl.ds(5 * nx, nx)], y1[pl.ds(5 * nx, nx)] = by_edge("gy", yp[5], ym[5])
        up = by_edge("gx", r0[5, ny - 1:ny], r1[5, ny - 1:ny])
        down = by_edge("gx", r0[5, 0:1], r1[5, 0:1])
        for n in range(2):
            at = pl.ds(6 * nx + n, 1)
            y0[at], y1[at] = by_edge("gy", up[1 - n], down[1 - n])
        rest = pl.ds(6 * nx + 2, 6)
        y0[rest] = y1[rest] = jnp.zeros((6, 128), jnp.float32)


def mark_x(r0, r1, flag_x0, flag_x1, hx):
    flags = by_edge("gx", flag_x0[5], flag_x1[5])
    for k in range(5):
        values = by_edge("gx", r0[k], r1[k])
        for side in range(2):
            hx[side, k] = jnp.where(flags[1 - side] > 0.5, MARK, values[1 - side])


def mark_y(s0, s1, flag_y0, flag_y1, hy):
    nx = hy.shape[2]
    row = lax.broadcasted_iota(jnp.int32, hy.shape[2:], 0)
    own = by_edge("gy", flag_y0[pl.ds(5 * nx, nx)], flag_y1[pl.ds(5 * nx, nx)])
    left, right = [
        by_edge("gy", flag_y0[pl.ds(6 * nx + n, 1)], flag_y1[pl.ds(6 * nx + n, 1)]) for n in range(2)
    ]
    for side, group in enumerate((YP, YM)):
        flags = {
            0: own[1 - side],
            1: jnp.where(row == 0, left[1 - side], pltpu.roll(own[1 - side], 1, 0)),
            -1: jnp.where(row == nx - 1, right[1 - side], pltpu.roll(own[1 - side], nx - 1, 0)),
        }
        for k in range(5):
            at = pl.ds(k * nx, nx)
            value = by_edge("gy", s0[at], s1[at])[1 - side]
            hy[side, k] = jnp.where(flags[VEL[group[k]][0]] > 0.5, MARK, value)


def arriving(post, hx, hy, x, t, i):
    nx, tiles = post.shape[1], post.shape[2] // 8
    cx, cy, cz = VEL[i]
    if isinstance(x, int) and not 0 <= x - cx < nx:
        view = hx.at[0, XP.index(i)] if cx == 1 else hx.at[1, XM.index(i)]
    else:
        view = post.at[i, x - cx]
    row = lax.broadcasted_iota(jnp.int32, (8, 128), 0)
    if cy == 1 and t == 0:
        v = pltpu.roll(view[pl.ds(0, 8), :], 1, 0)
        if hy is not None:
            v = jnp.where(row == 0, jnp.broadcast_to(hy[0, YP.index(i), pl.ds(x, 1), :], (8, 128)), v)
    elif cy == -1 and t == tiles - 1:
        v = pltpu.roll(view[pl.ds(8 * t, 8), :], 7, 0)
        if hy is not None:
            v = jnp.where(row == 7, jnp.broadcast_to(hy[1, YM.index(i), pl.ds(x, 1), :], (8, 128)), v)
    else:
        v = view[pl.ds(8 * t - cy, 8), :]
    return pltpu.roll(v, cz % 128, 1) if cz else v


def stream(post, hx, hy, x, t):
    own = [post[i, x, pl.ds(8 * t, 8), :] for i in range(NQ)]
    f = [own[0]]
    for i in range(1, NQ):
        v = arriving(post, hx, hy, x, t, i)
        f.append(jnp.where(v < EDGE, own[opposite(i)], v))
    return f, own, own[0] > EDGE


def advance(post, hx, hy, x, t, out, faces):
    nx, tiles = post.shape[1], post.shape[2] // 8
    f, own, fluid = stream(post, hx, hy, x, t)
    new = collide(f)
    for i in range(NQ):
        out[i, x, pl.ds(8 * t, 8), :] = jnp.where(fluid, new[i], own[i])
    send_faces(x, t, nx - 1, tiles - 1, lambda group: [new[i] for i in group], *faces)


def centre_kernel(post, r0, r1, flag_x0, flag_x1, out, xp, xm, hx):
    nx, ny = post.shape[1], post.shape[2]
    mark_x(r0, r1, flag_x0, flag_x1, hx)

    def body(x):
        for t in range(1, ny // 8 - 1):
            advance(post, hx, None, x, t, out, (xp, xm, None, None))

    body(0)
    body(nx - 1)
    inner_columns(nx, body)


def edge_kernel(post, hx, xp_in, xm_in, s0, s1, flag_y0, flag_y1, out_in, out, x0, x1, yp, ym, hy, xp, xm):
    nx, ny = post.shape[1], post.shape[2]
    mark_y(s0, s1, flag_y0, flag_y1, hy)
    for x in (0, nx - 1):
        for t in (0, ny // 8 - 1):
            advance(post, hx, hy, x, t, out, (xp, xm, yp, ym))
    for rows, up, down in (
        (pl.ds(0, 8), xp, xm),
        (pl.ds(8, ny - 16), xp_in, xm_in),
        (pl.ds(ny - 8, 8), xp, xm),
    ):
        for k in range(5):
            x0[k, rows, :], x1[k, rows, :] = by_edge("gx", up[k, rows, :], down[k, rows, :])


def rim_kernel(post, hy, out_in, yp_in, ym_in, out, yp, ym):
    def body(x):
        for t in (0, post.shape[2] // 8 - 1):
            advance(post, None, hy, x, t, out, (None, None, yp, ym))

    inner_columns(post.shape[1], body, 2)


def last_centre_kernel(post, r0, r1, flag_x0, flag_x1, out_hbm, hx, stage, sem):
    nx, ny = post.shape[1], post.shape[2]
    mark_x(r0, r1, flag_x0, flag_x1, hx)

    def body(x):
        for t in range(ny // 8):
            f, own, fluid = stream(post, hx, None, x, t)
            for i in range(NQ):
                stage[i, x, pl.ds(8 * t, 8), :] = jnp.where(fluid, f[i], own[i] * (1.0 / MARK))

    def step(x, carry):
        body(x)
        return carry

    parts = sem.shape[0]
    size = nx // parts
    copies = []
    for p in range(parts):
        low, high = p * size, (p + 1) * size
        if p == 0:
            body(0)
        lax.fori_loop(max(low, 1), min(high, nx - 1), step, 0)
        if p == parts - 1:
            body(nx - 1)
        at = pl.ds(low, size)
        copies.append(pltpu.make_async_copy(stage.at[:, at], out_hbm.at[:, at], sem.at[p]))
        copies[-1].start()
    for copy in copies:
        copy.wait()


def last_kernel(post, hx, s0, s1, flag_y0, flag_y1, out_in, out_hbm, stage, hy, sem):
    nx, ny = post.shape[1], post.shape[2]
    mark_y(s0, s1, flag_y0, flag_y1, hy)
    copies = []
    for side, (t, group) in enumerate(((0, YP), (ny // 8 - 1, YM))):
        rows = pl.ds(8 * t, 8)
        fluid = [post[0, x, rows, :] > EDGE for x in range(nx)]
        for k, i in enumerate(group):
            for x in range(nx):
                v = arriving(post, hx, hy, x, t, i)
                v = jnp.where(v < EDGE, post[opposite(i), x, rows, :], v)
                stage[side, k, x] = jnp.where(fluid[x], v, post[i, x, rows, :] * (1.0 / MARK))
            copies.append(pltpu.make_async_copy(stage.at[side, k], out_hbm.at[i, :, rows], sem.at[side, k]))
            copies[-1].start()
    for copy in copies:
        copy.wait()


def swap(value, axis, edge):
    count = lax.axis_size(axis)
    pairs = [((2 * j + edge) % count, (2 * j + edge + 1) % count) for j in range(count // 2)]
    return lax.ppermute(value, axis, pairs + [(b, a) for a, b in pairs])


def local(populations, solid):
    _, nx, ny, nz = populations.shape
    f32 = jnp.float32
    anywhere = pl.BlockSpec(memory_space=pl.ANY)
    onchip = pl.BlockSpec(memory_space=pltpu.VMEM)
    state = pltpu.VMEM(populations.shape, f32)
    params = pltpu.CompilerParams(vmem_limit_bytes=24 << 20)

    def kernel(body, out_shape, in_specs, out_specs=None, scratch=(), aliases={}):
        return pl.pallas_call(
            body,
            out_shape=out_shape,
            in_specs=in_specs,
            out_specs=out_specs or (onchip,) * len(out_shape),
            scratch_shapes=list(scratch),
            input_output_aliases=aliases,
            compiler_params=params,
            cost_estimate=pl.CostEstimate(flops=1 << 24, bytes_accessed=1 << 22, transcendentals=0),
        )

    def held(value):
        return pltpu.with_memory_space_constraint(value, pltpu.VMEM)

    def face_x(planes):
        return jax.ShapeDtypeStruct((planes, ny, nz), f32)

    def face_y(planes):
        return jax.ShapeDtypeStruct((planes, nx, nz), f32)

    def swap_x(x0, x1):
        return swap(x0, "gx", 0), swap(x1, "gx", 1)

    def swap_y(yp, ym, r0, r1):
        rows = 5 * nx if yp.shape[0] == 5 else 6 * nx + 8
        shape = jax.ShapeDtypeStruct((rows, nz), f32)
        y0, y1 = kernel(corner_kernel, (shape,) * 2, [onchip] * 4)(yp, ym, r0, r1)
        return swap(y0, "gy", 0), swap(y1, "gy", 1)

    post, x0, x1, yp, ym = kernel(
        first_edge_kernel,
        (state, face_x(6), face_x(6), face_y(6), face_y(6)),
        [anywhere] * 2,
        scratch=[pltpu.VMEM((6, ny, nz), f32)] * 2
        + [pltpu.VMEM(solid.shape, jnp.int32), pltpu.SemaphoreType.DMA((4,))],
    )(
        pltpu.with_memory_space_constraint(populations, pltpu.HBM),
        pltpu.with_memory_space_constraint(solid, pltpu.HBM),
    )
    r0, r1 = swap_x(x0, x1)
    post, yp, ym = kernel(
        first_inner_kernel, (state, face_y(6), face_y(6)), [onchip] * 5, aliases={2: 0, 3: 1, 4: 2}
    )(held(populations), held(solid), held(post), yp, ym)
    flag_x = (r0, r1)
    s0, s1 = flag_y = swap_y(yp, ym, r0, r1)
    marked_x = jax.ShapeDtypeStruct((2, 5, ny, nz), f32)
    marked_y = jax.ShapeDtypeStruct((2, 5, nx, nz), f32)
    for _ in range(1, ITERS):
        post = held(post)
        new, xp, xm, hx = kernel(
            centre_kernel, (state, face_x(5), face_x(5), marked_x), [onchip] * 5
        )(post, r0, r1, *flag_x)
        new, x0, x1, yp, ym, hy = kernel(
            edge_kernel,
            (state, face_x(5), face_x(5), face_y(5), face_y(5), marked_y),
            [onchip] * 9,
            scratch=[pltpu.VMEM((5, ny, nz), f32)] * 2,
            aliases={8: 0},
        )(post, hx, xp, xm, s0, s1, *flag_y, held(new))
        r0, r1 = swap_x(x0, x1)
        new, yp, ym = kernel(
            rim_kernel, (state, face_y(5), face_y(5)), [onchip] * 5, aliases={2: 0, 3: 1, 4: 2}
        )(post, hy, held(new), yp, ym)
        s0, s1 = swap_y(yp, ym, r0, r1)
        post = new
    post = held(post)
    whole = jax.ShapeDtypeStruct(populations.shape, f32)
    out, hx = kernel(
        last_centre_kernel,
        (whole, marked_x),
        [onchip] * 5,
        (anywhere, onchip),
        scratch=[pltpu.VMEM(populations.shape, f32), pltpu.SemaphoreType.DMA((4,))],
    )(post, r0, r1, *flag_x)
    (out,) = kernel(
        last_kernel,
        (whole,),
        [onchip] * 6 + [anywhere],
        (anywhere,),
        scratch=[
            pltpu.VMEM((2, 5, nx, 8, nz), f32),
            pltpu.VMEM((2, 5, nx, nz), f32),
            pltpu.SemaphoreType.DMA((2, 5)),
        ],
        aliases={6: 0},
    )(post, hx, s0, s1, *flag_y, out)
    return out


def solution(mesh):
    in_specs = (P(None, "gx", "gy", None), P("gx", "gy", None))
    out_specs = P(None, "gx", "gy", None)
    return jax.shard_map(local, mesh=mesh, in_specs=in_specs, out_specs=out_specs, check_vma=False)
```
